32 devices in a mesh: space: 4 (over x, core), mem: 8 (over z, y).
Axes of the slice: x: 2, y: 2, z: 4, core: 2. Of those that a mesh axis runs over, the one named last changes fastest.
Arguments:
- prior_ensemble: float32 [512, 8192], P('mem', 'space'), may hold values from -5 to 5
- terminal_particles: float32 [512, 8192], P(None, ('space', 'mem')), may hold values from -5 to 5
- reverse_perturbation: float32 [3, 512, 8192], P(None, None, ('space', 'mem')), may hold values from -6 to 6
- measured_angles: float32 [8192], P(('space', 'mem')), may hold values from -1.3 to 1.3
Outputs:
- analysis: float32 [512, 8192], P(None, ('space', 'mem'))
The draws below stay inside these ranges and needn't reach their ends.
All inputs are finite; a program needn't handle non-finite values.
Results may differ from the reference program's by a relative error of at most 0.0003.
Values sent between devices are 32-bit elements; how exact they have to be, the bound alone decides.
A program may use at most 64 MiB of HBM per device.

```python
import math
import jax
import jax.numpy as jnp
from jax import lax

M = 512
S = 512
ITERS = 3
V = 8192


def member_field(key):
    base = jax.random.fold_in(key, 7)
    first = jax.random.fold_in(base, 0)
    return jnp.clip(jax.random.normal(first, (M, V), jnp.float32), -5.0, 5.0)


def draw_prior_ensemble(key, part):
    return member_field(key).astype(jnp.float32)


def draw_terminal_particles(key, part):
    base = jax.random.fold_in(key, 11)
    return jnp.clip(jax.random.normal(base, (S, V), jnp.float32), -5.0, 5.0)


def block_levels(rng, extent, pieces, low, largest):
    def one(position, shards_of):
        steps = jax.random.uniform(jax.random.fold_in(jax.random.fold_in(rng, 6), position), (shards_of,), jnp.float32, low / len(pieces), largest / len(pieces))
        return jnp.repeat(jnp.exp(steps), extent[position] // shards_of).reshape((-1,) + (1,) * (len(extent) - position - 1))

    factor_of = one(*pieces[0])
    for cut in pieces[1:]:
        factor_of = factor_of * one(*cut)
    return factor_of


def noise(key, shape, scale, reach, pieces=(), kind=jnp.bfloat16):
    array = scale * jax.random.normal(key, shape, jnp.float32)
    if pieces:
        array = array * block_levels(key, shape, pieces, -0.22, 0.18)
    return jnp.clip(array, -reach, reach).astype(kind)


def setup_inputs(seed: int = 0) -> dict:
    key_list = jax.random.split(jax.random.key(seed), 5)
    prior_ensemble = draw_prior_ensemble(jax.random.fold_in(key_list[4], 71), 0)
    terminal_particles = draw_terminal_particles(jax.random.fold_in(key_list[4], 71), 0)
    reverse_perturbation = noise(key_list[2], (ITERS, S, V), 1.0, 6.0, ((2, 32),), jnp.float32)
    measured_angles = jnp.clip(jax.random.uniform(key_list[3], (V,), jnp.float32, -1.3, 1.3) * block_levels(key_list[3], (V,), ((0, 32),), -0.4, 0.0), -1.3, 1.3)
    return {"prior_ensemble": prior_ensemble, "terminal_particles": terminal_particles, "reverse_perturbation": reverse_perturbation, "measured_angles": measured_angles}


def reference(prior_ensemble, terminal_particles, reverse_perturbation, measured_angles):
    peak_log_likelihood = lax.Precision.HIGHEST
    particle_lengths = lax.optimization_barrier(jnp.sum(prior_ensemble * prior_ensemble, axis=1))
    temper = math.sqrt(V)
    gaussian_variates = terminal_particles
    for step in range(ITERS):
        t = 1.0 - step / ITERS
        dt = 1.0 / ITERS
        alpha = 1.0 - 0.5 * t
        sigma2 = t
        drift = -0.5 / alpha
        g2 = 1.0 + t / alpha
        damp = 1.0 - t
        inner_pairing_matrix = jnp.dot(gaussian_variates, prior_ensemble.T, precision=peak_log_likelihood, preferred_element_type=jnp.float32)
        logits = (2.0 * alpha * inner_pairing_matrix - alpha * alpha * particle_lengths[None, :]) / (2.0 * sigma2 * temper)
        annealed_importance = jax.nn.softmax(logits, axis=1)
        mixed_correction = jnp.dot(annealed_importance, prior_ensemble, precision=peak_log_likelihood, preferred_element_type=jnp.float32)
        score = -(gaussian_variates - alpha * mixed_correction) / sigma2 + damp * 4.0 * (measured_angles[None, :] - jnp.arctan(gaussian_variates)) / (1.0 + gaussian_variates * gaussian_variates)
        gaussian_variates = gaussian_variates + dt * (-drift * gaussian_variates + g2 * score) + math.sqrt(dt * g2) * reverse_perturbation[step]
    return gaussian_variates
```

```python
import functools
import math

import jax
import jax.numpy as jnp
from jax import lax
from jax.experimental import pallas as pl
from jax.experimental.pallas import tpu as pltpu
from jax.sharding import PartitionSpec as P

ITERS = 3
CHUNKS = 4
CORES = 2
SUBLANES = 8
SQUARE = 3
SETS = 4
LANES = 128
MESH = pl.DeviceIdType.MESH


def split(a, parts):
    out = []
    for _ in range(parts):
        out.append(a.astype(jnp.bfloat16))
        a = a - out[-1].astype(jnp.float32)
    return out


def product(a, parts, contract_b):
    n = a.shape[0]
    lhs = split(a, len(parts))
    total = None
    for i in reversed(range(len(parts))):
        rows = lhs[: len(parts) - i]
        both = lax.dot_general(
            jnp.concatenate(rows, axis=0),
            parts[i],
            (((1,), (contract_b,)), ((), ())),
            preferred_element_type=jnp.float32,
        )
        for j in reversed(range(len(rows))):
            term = both[j * n : (j + 1) * n]
            total = term if total is None else total + term
    return total


def arctan(x):
    a = jnp.abs(x)
    big = a > 2.414213562373095
    mid = a > 0.4142135623730950
    num = jnp.where(big, -1.0, jnp.where(mid, a - 1.0, a))
    den = jnp.where(big, a, jnp.where(mid, a + 1.0, 1.0))
    base = jnp.where(big, math.pi / 2, jnp.where(mid, math.pi / 4, 0.0))
    r = num / den
    s = r * r
    poly = ((8.05374449538e-2 * s - 1.38776856032e-1) * s + 1.99777106478e-1) * s
    poly = (poly - 3.33329491539e-1) * s * r + r
    y = base + poly
    return jnp.where(x < 0.0, -y, y)


def rows_at(start, size):
    return pl.ds(pl.multiple_of(start, SUBLANES), size)


def constants(k):
    t = 1.0 - k / ITERS
    alpha = 1.0 - 0.5 * t
    return t, alpha, -0.5 / alpha, 1.0 + t / alpha, 1.0 - t


def kernel(
    plan,
    prior,
    terminal,
    perturbation,
    angles,
    out,
    x,
    z,
    noise,
    seen,
    gram,
    xy_in,
    part,
    z_in,
    numer,
    w,
    square,
    xb,
    kb,
    pull,
    send,
    recv,
    give_send,
    give_recv,
    once_send,
    once_recv,
    local,
):
    n_space, n_mem, ny, nz, scatter_z, mixed, temper = plan
    nxy = (n_space // CORES) * ny
    _, chunks, rows, _ = gram.shape
    rows3 = rows // nxy
    samples = z.shape[0]
    members = prior.shape[0]
    variables = terminal.shape[1]
    lanes = numer.shape[4]
    dt = 1.0 / ITERS

    sp = lax.axis_index("space")
    me = lax.axis_index("mem")
    core = lax.rem(sp, CORES)
    other = 1 - core
    xi = lax.div(sp, CORES)
    yi = lax.rem(me, ny)
    zi = lax.div(me, ny)

    core_dev = (xi * CORES + other, me)

    here = {"x": xi, "y": yi, "z": zi, "one": 0}
    size = {"x": n_space // CORES, "y": ny, "z": nz, "one": 1}

    def position(axes):
        return here[axes[0]] * size[axes[1]] + here[axes[1]]

    def peer(axes, d):
        p = lax.rem(position(axes) + d, size[axes[0]] * size[axes[1]])
        at = dict(here)
        at[axes[0]] = lax.div(p, size[axes[1]])
        at[axes[1]] = lax.rem(p, size[axes[1]])
        return p, (at["x"] * CORES + core, at["z"] * ny + at["y"])

    orders = [(("x", "y"), ("one", "z"))]
    if mixed:
        orders += [orders[0][::-1], orders[0], orders[0]]
    orders = [orders[c % len(orders)] for c in range(chunks)]

    def mem_peer(d):
        p = lax.rem(me + d, n_mem)
        return p, (sp, p)

    def cols(p):
        return pl.ds(pl.multiple_of(p * variables, variables), variables)

    mine = cols(core)
    my_samples = rows_at(core * samples, samples)
    its_samples = rows_at(other * samples, samples)
    my_members = rows_at(me * members, members)

    loads = [
        pltpu.make_async_copy(
            prior.at[:, cols(me)], x.at[my_members, mine], local.at[0]
        ),
        pltpu.make_async_copy(terminal.at[my_samples, :], z.at[:, mine], local.at[1]),
        pltpu.make_async_copy(angles, seen.at[:, mine], local.at[2]),
        pltpu.make_async_copy(
            perturbation.at[:, my_samples, :], noise.at[:, :, mine], local.at[3]
        ),
    ]
    for copy in loads:
        copy.start()

    barrier = pltpu.get_barrier_semaphore()
    greet = [core_dev]
    for axes in sorted({axes for order in orders for axes in order}):
        n = size[axes[0]] * size[axes[1]]
        greet += [peer(axes, d)[1] for d in range(1, n)]
    greet += [mem_peer(d)[1] for d in range(1, n_mem)]
    for dev in greet:
        pl.semaphore_signal(barrier, inc=1, device_id=dev, device_id_type=MESH)
    pl.semaphore_wait(barrier, len(greet))

    def put_once(src, dst, i, dev):
        copy = pltpu.make_async_remote_copy(
            src_ref=src,
            dst_ref=dst,
            send_sem=once_send.at[i],
            recv_sem=once_recv.at[i],
            device_id=dev,
            device_id_type=MESH,
        )
        copy.start()
        return copy

    exchange = []
    for d in range(1, n_mem):
        p, dev = mem_peer(d)
        exchange.append(put_once(prior.at[:, cols(p)], x.at[my_members, mine], d - 1, dev))
    i = n_mem - 1
    swaps = [
        put_once(terminal.at[its_samples, :], z.at[:, mine], i, core_dev),
        put_once(angles, seen.at[:, mine], i + 1, core_dev),
        put_once(prior.at[:, cols(me)], x.at[my_members, mine], i + 2, core_dev),
        put_once(perturbation.at[:, its_samples, :], noise.at[:, :, mine], i + 3, core_dev),
    ]
    i = i + 4
    for d, copy in enumerate(exchange):
        copy.wait_recv()
        theirs = rows_at(lax.rem(me + n_mem - d - 1, n_mem) * members, members)
        swaps.append(put_once(x.at[theirs, mine], x.at[theirs, mine], i + d, core_dev))
    i = i + n_mem - 1
    for copy in loads[:3]:
        copy.wait()
    for copy in swaps[:3] + swaps[4:]:
        copy.wait_recv()

    xs = x[...]
    for j, piece in enumerate(split(xs, 3)):
        xb[j] = piece
    norms = jnp.zeros((SUBLANES, xs.shape[0]), jnp.float32)
    for piece in reversed(split(xs * xs, 3)):
        norms = norms + lax.dot_general(
            jnp.ones((SUBLANES, xs.shape[1]), jnp.bfloat16),
            piece,
            (((1,), (1,)), ((), ())),
            preferred_element_type=jnp.float32,
        )
    norms = norms[:1]

    all_sent = []
    inbound = {}
    first_z = nxy - 1
    first_gz = first_z + nz - 1

    def chunk_rows(c):
        return pl.ds(c * rows, rows)

    def owned(c):
        return rows_at(position(orders[c][0]) * rows3, rows3)

    def remote(src, dst, sent, got, dev):
        copy = pltpu.make_async_remote_copy(
            src_ref=src,
            dst_ref=dst,
            send_sem=sent,
            recv_sem=got,
            device_id=dev,
            device_id_type=MESH,
        )
        copy.start()
        all_sent.append(copy)
        return copy

    def put(s, c, i, src, dst, dev):
        return remote(src, dst, send.at[s, c, i], recv.at[s, c, i], dev)

    def scatter(s, c, value):
        gram[s, c] = value
        first = orders[c][0]
        group = []
        for d in range(1, nxy):
            p, dev = peer(first, d)
            src = gram.at[s, c, rows_at(p * rows3, rows3), :]
            group.append(put(s, c, d - 1, src, xy_in.at[s, c, d - 1], dev))
        inbound[s, c] = group

    def scatter_gram(k, c):
        alpha = constants(k)[1]
        inner = product(z[chunk_rows(c), :], [xb[0], xb[1], xb[2]], 1)
        scatter(k, c, 2.0 * alpha * inner - alpha * alpha * norms)

    def scatter_square(c):
        at = rows_at(core * samples + c * rows, rows)
        scatter(SQUARE, c, product(x[at, :], [xb[0], xb[1], xb[2]], 1))

    def second(s, c):
        after = orders[c][1]
        total = gram[s, c, owned(c), :]
        for d, copy in enumerate(inbound[s, c]):
            copy.wait_recv()
            total = total + xy_in[s, c, d]
        if scatter_z:
            for p in range(nz):
                part[s, c, p] = total[:, p * lanes : (p + 1) * lanes]
        else:
            part[s, c, 0] = total
        group = []
        for d in range(1, nz):
            p, dev = peer(after, d)
            src = part.at[s, c, p] if scatter_z else part.at[s, c, 0]
            group.append(put(s, c, first_z + d - 1, src, z_in.at[s, c, d - 1], dev))
        inbound[s, c] = group

    def third(s, c):
        after = orders[c][1]
        z_at = position(after) if scatter_z else 0
        block = part[s, c, z_at]
        for d, copy in enumerate(inbound[s, c]):
            copy.wait_recv()
            block = block + z_in[s, c, d]
        numer[s, c, z_at] = block
        inbound[s, c] = []
        if scatter_z:
            at = numer.at[s, c, z_at]
            inbound[s, c] = [
                put(s, c, first_gz + d - 1, at, at, peer(after, d)[1]) for d in range(1, nz)
            ]

    def full(s, c):
        for copy in inbound[s, c]:
            copy.wait_recv()
        if scatter_z:
            return jnp.concatenate([numer[s, c, p] for p in range(nz)], axis=1)
        return numer[s, c, 0]

    def share(s, c, at):
        first = orders[c][0]
        inbound["share", s, c] = [
            remote(at, at, give_send.at[s, c, d - 1], give_recv.at[s, c, d - 1], peer(first, d)[1])
            for d in range(1, nxy)
        ]

    def arrived(s, c):
        for copy in inbound["share", s, c]:
            copy.wait_recv()

    def share_weights(k, c, block):
        logits = block / (2.0 * constants(k)[0] * temper)
        e = jnp.exp(logits - jnp.max(logits, axis=1, keepdims=True))
        w[k, c, owned(c), :] = e / jnp.sum(e, axis=1, keepdims=True)
        share(k, c, w.at[k, c, owned(c), :])

    def share_square(c):
        at = rows_at(core * samples + c * rows + position(orders[c][0]) * rows3, rows3)
        square[at, :] = full(SQUARE, c)
        share(SQUARE, c, square.at[at, :])

    def advance(k, c):
        t, alpha, drift, g2, damp = constants(k)
        where = chunk_rows(c)
        zs = z[where, :]
        seen_term = damp * 4.0 * (seen[...] - arctan(zs)) / (1.0 + zs * zs)
        z[where, :] = (
            zs
            + dt * (-drift * zs + g2 * (seen_term - zs / t))
            + math.sqrt(dt * g2) * noise[k, where, :]
        )

    def add_blend(k, c):
        t, alpha, _, g2, _ = constants(k)
        where = chunk_rows(c)
        arrived(k, c)
        blend = product(w[k, c], [xb[0], xb[1]], 0)
        z[where, :] = z[where, :] + (dt * g2 * alpha / t) * blend

    def pull_on(k):
        t, alpha, _, g2, _ = constants(k)
        scale = 2.0 * constants(k + 1)[1] * (dt * g2 * alpha / t)
        mine_w = jnp.concatenate([w[k, c, owned(c), :] for c in range(chunks)], axis=0)
        pull[k] = scale * product(mine_w, [kb[0], kb[1], kb[2]], 0)

    each = range(chunks)
    for c in each:
        scatter_gram(0, c)
    for c in each:
        scatter_square(c)
    loads[3].wait()
    swaps[3].wait_recv()
    for c in each:
        advance(0, c)
        scatter_gram(1, c)
    for c in each:
        second(0, c)
    for c in each:
        second(SQUARE, c)
    for c in each:
        third(0, c)
    for c in each:
        second(1, c)
    for c in each:
        share_weights(0, c, full(0, c))
    for c in each:
        third(SQUARE, c)
    for c in each:
        third(1, c)
    for c in each:
        share_square(c)
    for c in each:
        add_blend(0, c)
        advance(1, c)
        scatter_gram(2, c)
    halves = []
    for c in each:
        arrived(SQUARE, c)
        at = square.at[rows_at(core * samples + c * rows, rows), :]
        halves.append(put_once(at, at, i + c, core_dev))
    i = i + chunks
    for c in each:
        second(2, c)
    for copy in halves:
        copy.wait_recv()
    for j, piece in enumerate(split(square[...], 3)):
        kb[j] = piece
    pull_on(0)
    for c in each:
        share_weights(1, c, full(1, c) + pull[0, pl.ds(c * rows3, rows3), :])
    pull_on(1)
    for c in each:
        third(2, c)
    for c in each:
        add_blend(1, c)
        advance(2, c)
    for c in each:
        share_weights(2, c, full(2, c) + pull[1, pl.ds(c * rows3, rows3), :])
    results = []
    for c in each:
        add_blend(2, c)
        where = chunk_rows(c)
        target = out.at[rows_at(core * samples + c * rows, rows), :]
        result = pltpu.make_async_copy(z.at[where, mine], target, local.at[4 + c])
        result.start()
        results.append(result)
        swaps.append(put_once(z.at[where, cols(other)], target, i + c, core_dev))
    for copy in results:
        copy.wait()
    for copy in swaps[-chunks:]:
        copy.wait_recv()
    for copy in exchange + swaps + halves + all_sent:
        copy.wait_send()


def per_device(prior, terminal, perturbation, angles):
    n_space, n_mem = lax.axis_size("space"), lax.axis_size("mem")
    samples, variables = terminal.shape
    members = prior.shape[0] * n_mem
    assert members == samples
    nx = n_space // CORES
    ny = math.gcd(nx, n_mem)
    nz = n_mem // ny
    nxy = nx * ny
    half = samples // CORES
    chunks = CHUNKS
    while chunks > 1 and half % (chunks * nxy * SUBLANES):
        chunks //= 2
    rows = half // chunks
    rows3 = rows // nxy
    scatter_z = members % (nz * LANES) == 0
    pieces = nz if scatter_z else 1
    lanes = members // pieces
    mixed = nxy == nz and scatter_z
    temper = math.sqrt(variables * n_space * n_mem)
    f32 = jnp.float32
    exchanges = nxy - 1 + 2 * (nz - 1)
    once = 2 * (n_mem - 1) + 4 + 2 * chunks
    iters = perturbation.shape[0]
    anywhere = pl.BlockSpec(memory_space=pl.ANY)
    return pl.pallas_call(
        functools.partial(kernel, (n_space, n_mem, ny, nz, scatter_z, mixed, temper)),
        out_shape=jax.ShapeDtypeStruct((samples, variables), f32),
        in_specs=[anywhere] * 4,
        out_specs=anywhere,
        scratch_shapes=[
            pltpu.VMEM((members, CORES * variables), f32),
            pltpu.VMEM((half, CORES * variables), f32),
            pltpu.VMEM((iters, half, CORES * variables), f32),
            pltpu.VMEM((1, CORES * variables), f32),
            pltpu.VMEM((SETS, chunks, rows, members), f32),
            pltpu.VMEM((SETS, chunks, nxy - 1, rows3, members), f32),
            pltpu.VMEM((SETS, chunks, pieces, rows3, lanes), f32),
            pltpu.VMEM((SETS, chunks, nz - 1, rows3, lanes), f32),
            pltpu.VMEM((SETS, chunks, pieces, rows3, lanes), f32),
            pltpu.VMEM((iters, chunks, rows, members), f32),
            pltpu.VMEM((members, members), f32),
            pltpu.VMEM((3, members, CORES * variables), jnp.bfloat16),
            pltpu.VMEM((3, members, members), jnp.bfloat16),
            pltpu.VMEM((iters - 1, chunks * rows3, members), f32),
            pltpu.SemaphoreType.DMA((SETS, chunks, exchanges)),
            pltpu.SemaphoreType.DMA((SETS, chunks, exchanges)),
            pltpu.SemaphoreType.DMA((SETS, chunks, nxy - 1)),
            pltpu.SemaphoreType.DMA((SETS, chunks, nxy - 1)),
            pltpu.SemaphoreType.DMA((once,)),
            pltpu.SemaphoreType.DMA((once,)),
            pltpu.SemaphoreType.DMA((4 + chunks,)),
        ],
        compiler_params=pltpu.CompilerParams(collective_id=0, has_side_effects=True),
    )(prior, terminal, perturbation, angles.reshape(1, variables))


def solution(mesh):
    in_specs = (
        P("mem", "space"),
        P(None, ("space", "mem")),
        P(None, None, ("space", "mem")),
        P(("space", "mem")),
    )
    out_specs = P(None, ("space", "mem"))
    return jax.shard_map(
        per_device, mesh=mesh, in_specs=in_specs, out_specs=out_specs, check_vma=False
    )
```

```python
import functools
import math

import jax
import jax.numpy as jnp
from jax import lax
from jax.experimental import pallas as pl
from jax.experimental.pallas import tpu as pltpu
from jax.sharding import PartitionSpec as P

ITERS = 3
CHUNKS = 2
PARTS = 2
VMEM_LIMIT = 48 << 20
CORES = 2
SUBLANES = 8
LANES = 128
MESH = pl.DeviceIdType.MESH


def split(a, parts):
    out = []
    for _ in range(parts):
        out.append(a.astype(jnp.bfloat16))
        a = a - out[-1].astype(jnp.float32)
    return out


def product(a, parts, contract_b):
    n = a.shape[0]
    lhs = split(a, len(parts))
    total = None
    for i in reversed(range(len(parts))):
        rows = lhs[: len(parts) - i]
        both = lax.dot_general(
            jnp.concatenate(rows, axis=0),
            parts[i],
            (((1,), (contract_b,)), ((), ())),
            preferred_element_type=jnp.float32,
        )
        for j in reversed(range(len(rows))):
            term = both[j * n : (j + 1) * n]
            total = term if total is None else total + term
    return total


def arctan(x):
    a = jnp.abs(x)
    big = a > 2.414213562373095
    mid = a > 0.4142135623730950
    num = jnp.where(big, -1.0, jnp.where(mid, a - 1.0, a))
    den = jnp.where(big, a, jnp.where(mid, a + 1.0, 1.0))
    base = jnp.where(big, math.pi / 2, jnp.where(mid, math.pi / 4, 0.0))
    r = num / den
    s = r * r
    poly = ((8.05374449538e-2 * s - 1.38776856032e-1) * s + 1.99777106478e-1) * s
    poly = (poly - 3.33329491539e-1) * s * r + r
    y = base + poly
    return jnp.where(x < 0.0, -y, y)


def rows_at(start, size):
    return pl.ds(pl.multiple_of(start, SUBLANES), size)


def constants(k):
    t = 1.0 - k / ITERS
    alpha = 1.0 - 0.5 * t
    return t, alpha, -0.5 / alpha, 1.0 + t / alpha, 1.0 - t


def kernel(
    plan,
    prior,
    terminal,
    perturbation,
    angles,
    out,
    x,
    z,
    noise,
    seen,
    gram,
    sums,
    w,
    xb,
    sum_send,
    sum_recv,
    give_send,
    give_recv,
    once_send,
    once_recv,
    local,
):
    n_space, n_mem, scatter, temper = plan
    _, chunks, rows, members = gram.shape
    own_rows = rows // n_mem if scatter else rows
    samples = z.shape[0]
    block = prior.shape[0]
    variables = terminal.shape[1]
    nx = n_space // CORES
    dt = 1.0 / ITERS

    sp = lax.axis_index("space")
    me = lax.axis_index("mem")
    core = lax.rem(sp, CORES)
    xi = lax.div(sp, CORES)
    partner = (xi * CORES + 1 - core, me)

    def space_at(d):
        return lax.rem(sp + d + n_space, n_space)

    def x_at(d):
        return lax.rem(xi + d + nx, nx) * CORES + core

    def mem_to(d):
        if n_mem & (n_mem - 1):
            return lax.rem(me + d, n_mem)
        return flipped(d)

    def mem_from(d):
        if n_mem & (n_mem - 1):
            return lax.rem(me + n_mem - d, n_mem)
        return flipped(d)

    def flipped(d):
        p = me
        bit = 1
        while bit < n_mem:
            if d & bit:
                p = p + bit - 2 * bit * lax.rem(lax.div(me, bit), 2)
            bit *= 2
        return p

    def cols(p):
        return pl.ds(pl.multiple_of(p * variables, variables), variables)

    def block_rows(p):
        return rows_at(p * block, block)

    def sample_rows(p):
        return rows_at(p * samples, samples)

    loads = [
        pltpu.make_async_copy(prior.at[:, cols(me)], x.at[block_rows(me), cols(sp)], local.at[0]),
        pltpu.make_async_copy(terminal.at[sample_rows(sp), :], z.at[:, cols(sp)], local.at[1]),
        pltpu.make_async_copy(angles, seen.at[:, cols(sp)], local.at[2]),
        pltpu.make_async_copy(
            perturbation.at[:, sample_rows(sp), :], noise.at[:, :, cols(sp)], local.at[3]
        ),
    ]
    for copy in loads:
        copy.start()

    barrier = pltpu.get_barrier_semaphore()
    greet = [(space_at(d), me) for d in range(1, n_space)]
    greet += [(sp, mem_to(d)) for d in range(1, n_mem)]
    for dev in greet:
        pl.semaphore_signal(barrier, inc=1, device_id=dev, device_id_type=MESH)
    pl.semaphore_wait(barrier, len(greet))

    sent = []

    def remote(src, dst, out_sem, in_sem, dev):
        copy = pltpu.make_async_remote_copy(
            src_ref=src,
            dst_ref=dst,
            send_sem=out_sem,
            recv_sem=in_sem,
            device_id=dev,
            device_id_type=MESH,
        )
        copy.start()
        sent.append(copy)
        return copy

    used = [0]

    def put_once(src, dst, dev):
        i = used[0]
        used[0] += 1
        return remote(src, dst, once_send.at[i], once_recv.at[i], dev)

    here = x.at[block_rows(me), cols(sp)]
    exchange = [
        put_once(prior.at[:, cols(mem_to(d))], here, (sp, mem_to(d))) for d in range(1, n_mem)
    ]
    firsts = []
    for d in range(1, n_space):
        q = space_at(d)
        firsts.append(put_once(terminal.at[sample_rows(q), :], z.at[:, cols(sp)], (q, me)))
        firsts.append(put_once(angles, seen.at[:, cols(sp)], (q, me)))

    over_x, to_core = [], []

    def pass_on(src, at):
        over_x.append([put_once(src, at, (x_at(d), me)) for d in range(1, nx)])
        to_core.append(put_once(src, at, partner))

    pass_on(prior.at[:, cols(me)], here)
    for d, copy in enumerate(exchange, 1):
        copy.wait_recv()
        at = x.at[block_rows(mem_from(d)), cols(sp)]
        pass_on(at, at)
    onward = []
    for b, group in enumerate(over_x):
        origin = mem_from(b) if b else me
        for d, copy in enumerate(group, 1):
            copy.wait_recv()
            at = x.at[block_rows(origin), cols(x_at(-d))]
            onward.append(put_once(at, at, partner))
    for copy in loads[:3]:
        copy.wait()
    norms = jnp.zeros((SUBLANES, members), jnp.float32)

    def take(where):
        xs = x[:, where]
        for j, piece in enumerate(split(xs, PARTS)):
            xb[j, :, where] = piece
        total = jnp.zeros((SUBLANES, members), jnp.float32)
        for piece in reversed(split(xs * xs, 3)):
            total = total + lax.dot_general(
                jnp.ones((SUBLANES, xs.shape[1]), jnp.bfloat16),
                piece,
                (((1,), (1,)), ((), ())),
                preferred_element_type=jnp.float32,
            )
        return total

    for d in range(nx):
        norms = norms + take(cols(x_at(d)))
    for copy in to_core + onward + firsts:
        copy.wait_recv()
    for d in range(nx):
        norms = norms + take(cols(lax.rem(xi + d, nx) * CORES + 1 - core))
    norms = norms[:1]
    parts = [xb[j] for j in range(PARTS)]

    inbound = {}

    def chunk_rows(c):
        return pl.ds(c * rows, rows)

    def owned():
        return rows_at(me * own_rows, own_rows) if scatter else pl.ds(0, rows)

    def send_noise(k):
        return [
            put_once(
                perturbation.at[k, sample_rows(space_at(d)), :],
                noise.at[k, :, cols(sp)],
                (space_at(d), me),
            )
            for d in range(1, n_space)
        ]

    def send_sums(k, c):
        alpha = constants(k)[1]
        gram[k, c] = 2.0 * alpha * product(z[chunk_rows(c), :], parts, 1) - alpha * alpha * norms
        inbound["sums", k, c] = []
        for d in range(1, n_mem):
            p = mem_to(d)
            src = gram.at[k, c, rows_at(p * own_rows, own_rows), :] if scatter else gram.at[k, c]
            inbound["sums", k, c].append(
                remote(
                    src,
                    sums.at[k, c, d - 1],
                    sum_send.at[k, c, d - 1],
                    sum_recv.at[k, c, d - 1],
                    (sp, p),
                )
            )

    def send_weights(k, c):
        total = gram[k, c, owned(), :]
        for d, copy in enumerate(inbound["sums", k, c]):
            copy.wait_recv()
            total = total + sums[k, c, d]
        logits = total / (2.0 * constants(k)[0] * temper)
        e = jnp.exp(logits - jnp.max(logits, axis=1, keepdims=True))
        w[k, c, owned(), :] = e / jnp.sum(e, axis=1, keepdims=True)
        inbound["give", k, c] = []
        if scatter:
            at = w.at[k, c, owned(), :]
            inbound["give", k, c] = [
                remote(
                    at, at, give_send.at[k, c, d - 1], give_recv.at[k, c, d - 1], (sp, mem_to(d))
                )
                for d in range(1, n_mem)
            ]

    def advance(k, c):
        t, alpha, drift, g2, damp = constants(k)
        zs = z[chunk_rows(c), :]
        seen_term = damp * 4.0 * (seen[...] - arctan(zs)) / (1.0 + zs * zs)
        z[chunk_rows(c), :] = (
            zs
            + dt * (-drift * zs + g2 * (seen_term - zs / t))
            + math.sqrt(dt * g2) * noise[k, chunk_rows(c), :]
        )

    def add_blend(k, c):
        t, alpha, _, g2, _ = constants(k)
        for copy in inbound["give", k, c]:
            copy.wait_recv()
        blend = product(w[k, c], parts, 0)
        z[chunk_rows(c), :] = z[chunk_rows(c), :] + (dt * g2 * alpha / t) * blend

    each = list(range(chunks))
    results = []
    arriving = {}
    for k in range(ITERS):
        for c in each:
            if k > 0:
                add_blend(k - 1, c)
            send_sums(k, c)
        if k == 0:
            arriving[0] = send_noise(0)
        for c in each:
            send_weights(k, c)
        if k + 1 < ITERS:
            arriving[k + 1] = send_noise(k + 1)
        if k == 0:
            loads[3].wait()
        for copy in arriving[k]:
            copy.wait_recv()
        for c in each:
            advance(k, c)
    for c in each:
        add_blend(ITERS - 1, c)
        target = out.at[rows_at(sp * samples + c * rows, rows), :]
        results += [
            put_once(z.at[chunk_rows(c), cols(space_at(d))], target, (space_at(d), me))
            for d in range(1, n_space)
        ]
        own = pltpu.make_async_copy(z.at[chunk_rows(c), cols(sp)], target, local.at[4 + c])
        own.start()
        loads.append(own)
    for copy in loads[4:]:
        copy.wait()
    for copy in results:
        copy.wait_recv()
    for copy in sent:
        copy.wait_send()


def per_device(prior, terminal, perturbation, angles):
    n_space, n_mem = lax.axis_size("space"), lax.axis_size("mem")
    all_samples, variables = terminal.shape
    members = prior.shape[0] * n_mem
    samples = all_samples // n_space
    chunks = CHUNKS
    while chunks > 1 and samples % (chunks * n_mem * SUBLANES):
        chunks //= 2
    rows = samples // chunks
    scatter = rows % (n_mem * SUBLANES) == 0
    own_rows = rows // n_mem if scatter else rows
    wide = n_space * variables
    temper = math.sqrt(wide * n_mem)
    f32 = jnp.float32
    nx = n_space // CORES
    iters = perturbation.shape[0]
    once = n_mem - 1 + (2 + iters + chunks) * (n_space - 1) + n_mem * (2 * nx - 1)
    operands = prior, terminal, perturbation, angles.reshape(1, variables)
    anywhere = pl.BlockSpec(memory_space=pl.ANY)
    return pl.pallas_call(
        functools.partial(kernel, (n_space, n_mem, scatter, temper)),
        out_shape=jax.ShapeDtypeStruct((all_samples, variables), f32),
        in_specs=[anywhere] * 4,
        out_specs=anywhere,
        scratch_shapes=[
            pltpu.VMEM((members, wide), f32),
            pltpu.VMEM((samples, wide), f32),
            pltpu.VMEM((iters, samples, wide), f32),
            pltpu.VMEM((1, wide), f32),
            pltpu.VMEM((iters, chunks, rows, members), f32),
            pltpu.VMEM((iters, chunks, n_mem - 1, own_rows, members), f32),
            pltpu.VMEM((iters, chunks, rows, members), f32),
            pltpu.VMEM((PARTS, members, wide), jnp.bfloat16),
            pltpu.SemaphoreType.DMA((iters, chunks, n_mem - 1)),
            pltpu.SemaphoreType.DMA((iters, chunks, n_mem - 1)),
            pltpu.SemaphoreType.DMA((iters, chunks, n_mem - 1)),
            pltpu.SemaphoreType.DMA((iters, chunks, n_mem - 1)),
            pltpu.SemaphoreType.DMA((once,)),
            pltpu.SemaphoreType.DMA((once,)),
            pltpu.SemaphoreType.DMA((4 + chunks,)),
        ],
        compiler_params=pltpu.CompilerParams(
            collective_id=0, has_side_effects=True, vmem_limit_bytes=VMEM_LIMIT
        ),
    )(*[pltpu.with_memory_space_constraint(a, pltpu.HBM) for a in operands])


def solution(mesh):
    in_specs = (
        P("mem", "space"),
        P(None, ("space", "mem")),
        P(None, None, ("space", "mem")),
        P(("space", "mem")),
    )
    out_specs = P(None, ("space", "mem"))
    return jax.shard_map(
        per_device, mesh=mesh, in_specs=in_specs, out_specs=out_specs, check_vma=False
    )
```

```python
import functools
import math

import jax
import jax.numpy as jnp
from jax import lax
from jax.experimental import pallas as pl
from jax.experimental.pallas import tpu as pltpu
from jax.sharding import PartitionSpec as P

ITERS = 3
CHUNKS = 2
PARTS = 2
VMEM_LIMIT = 48 << 20
CORES = 2
SUBLANES = 8
LANES = 128
MESH = pl.DeviceIdType.MESH


def split(a, parts):
    out = []
    for _ in range(parts):
        out.append(a.astype(jnp.bfloat16))
        a = a - out[-1].astype(jnp.float32)
    return out


def product(a, parts, contract_b):
    n = a.shape[0]
    lhs = split(a, len(parts))
    total = None
    for i in reversed(range(len(parts))):
        rows = lhs[: len(parts) - i]
        both = lax.dot_general(
            jnp.concatenate(rows, axis=0),
            parts[i],
            (((1,), (contract_b,)), ((), ())),
            preferred_element_type=jnp.float32,
        )
        for j in reversed(range(len(rows))):
            term = both[j * n : (j + 1) * n]
            total = term if total is None else total + term
    return total


def arctan(x):
    a = jnp.abs(x)
    big = a > 2.414213562373095
    mid = a > 0.4142135623730950
    num = jnp.where(big, -1.0, jnp.where(mid, a - 1.0, a))
    den = jnp.where(big, a, jnp.where(mid, a + 1.0, 1.0))
    base = jnp.where(big, math.pi / 2, jnp.where(mid, math.pi / 4, 0.0))
    r = num / den
    s = r * r
    poly = ((8.05374449538e-2 * s - 1.38776856032e-1) * s + 1.99777106478e-1) * s
    poly = (poly - 3.33329491539e-1) * s * r + r
    y = base + poly
    return jnp.where(x < 0.0, -y, y)


def rows_at(start, size):
    return pl.ds(pl.multiple_of(start, SUBLANES), size)


def constants(k):
    t = 1.0 - k / ITERS
    alpha = 1.0 - 0.5 * t
    return t, alpha, -0.5 / alpha, 1.0 + t / alpha, 1.0 - t


def kernel(
    plan,
    prior,
    terminal,
    perturbation,
    angles,
    out,
    x,
    z,
    noise,
    seen,
    gram,
    sums,
    w,
    xb,
    xt,
    norms,
    send,
    recv,
    local,
):
    n_space, n_mem, scatter, temper = plan
    _, chunks, rows, members = gram.shape
    own_rows = rows // n_mem if scatter else rows
    samples = z.shape[0]
    block = prior.shape[0]
    variables = terminal.shape[1]
    nx = n_space // CORES
    dt = 1.0 / ITERS

    sp = lax.axis_index("space")
    me = lax.axis_index("mem")
    core = lax.rem(sp, CORES)
    xi = lax.div(sp, CORES)
    partner = (xi * CORES + 1 - core, me)

    def space_at(d):
        return lax.rem(sp + d + n_space, n_space)

    def x_at(d):
        return lax.rem(xi + d + nx, nx) * CORES + core

    def pair(d):
        p = me
        bit = 1
        while bit < n_mem:
            if d & bit:
                p = p + bit - 2 * bit * lax.rem(lax.div(me, bit), 2)
            bit *= 2
        return p

    def cols(p):
        return pl.ds(pl.multiple_of(p * variables, variables), variables)

    def block_rows(p):
        return rows_at(p * block, block)

    def chunk_rows(c):
        return pl.ds(c * rows, rows)

    def sample_rows(p):
        return rows_at(p * samples, samples)

    loads = [
        pltpu.make_async_copy(prior.at[:, cols(me)], x.at[sp, block_rows(me), :], local.at[0]),
        pltpu.make_async_copy(terminal.at[sample_rows(sp), :], z.at[:, cols(sp)], local.at[1]),
        pltpu.make_async_copy(angles, seen.at[:, cols(sp)], local.at[2]),
        pltpu.make_async_copy(
            perturbation.at[:, sample_rows(sp), :], noise.at[:, :, cols(sp)], local.at[3]
        ),
    ]
    for copy in loads:
        copy.start()

    barrier = pltpu.get_barrier_semaphore()
    greet = [(space_at(d), me) for d in range(1, n_space)]
    greet += [(sp, pair(d)) for d in range(1, n_mem)]
    for dev in greet:
        pl.semaphore_signal(barrier, inc=1, device_id=dev, device_id_type=MESH)
    pl.semaphore_wait(barrier, len(greet))

    together = max(1, LANES // block)
    groups = range(n_mem // together)
    slots = {}
    pending = {}

    def put(key, src, dst, dev):
        i = slots.setdefault(key, len(slots))
        if i in pending:
            pending[i].wait_send()
        pending[i] = pltpu.make_async_remote_copy(
            src_ref=src,
            dst_ref=dst,
            send_sem=send.at[i],
            recv_sem=recv.at[i],
            device_id=dev,
            device_id_type=MESH,
        )
        pending[i].start()
        return pending[i]

    here = x.at[sp, block_rows(me), :]
    exchange = {
        d: put(("mem", d), prior.at[:, cols(pair(d))], here, (sp, pair(d)))
        for d in range(1, n_mem)
    }

    def send_start(c):
        copies = []
        for d in range(1, n_space):
            q = space_at(d)
            src = terminal.at[rows_at(q * samples + c * rows, rows), :]
            copies.append(put(("space", c, d), src, z.at[chunk_rows(c), cols(sp)], (q, me)))
        return copies

    starts = [send_start(0)]

    over_x, to_core, onward = [], [], []

    def group_at(i):
        return rows_at(lax.div(pair(i * together), together) * together * block, together * block)

    def group_blocks(i):
        return range(i * together, (i + 1) * together)

    def pass_on(b, src, at):
        over_x.append(
            [put(("x", b, d), src, at, (x_at(d), me)) for d in range(1, nx)]
        )

    def pass_core(i):
        for b in group_blocks(i):
            for copy in over_x[b]:
                copy.wait_recv()
        onward.append([])
        for d in range(1, nx):
            at = x.at[x_at(-d), group_at(i), :]
            onward[i].append(put(("onward", i, d), at, at, partner))

    def take(q, i):
        some = group_at(i)
        xs = x[q, some, :]
        for j, piece in enumerate(split(xs, PARTS)):
            xb[j, some, cols(q)] = piece
        turned = xs.T
        for j, piece in enumerate(split(turned, PARTS)):
            xt[j, cols(q), some] = piece
        norms[:, some] = norms[:, some] + jnp.sum(turned * turned, axis=0, keepdims=True)

    norms[...] = jnp.zeros_like(norms)
    pass_on(0, prior.at[:, cols(me)], here)
    loads[0].wait()
    for i in groups:
        for d in group_blocks(i):
            if d:
                exchange[d].wait_recv()
                at = x.at[sp, block_rows(pair(d)), :]
                pass_on(d, at, at)
        at = x.at[sp, group_at(i), :]
        to_core.append(put(("core", i), at, at, partner))
        take(sp, i)
    starts += [send_start(c) for c in range(1, chunks)]
    firsts = [
        put(("angles", d), angles, seen.at[:, cols(sp)], (space_at(d), me))
        for d in range(1, n_space)
    ]
    for copy in loads[1:3]:
        copy.wait()

    inbound = {}

    def owned():
        return rows_at(me * own_rows, own_rows) if scatter else pl.ds(0, rows)

    def send_noise(k):
        return [
            put(
                ("noise", k, d),
                perturbation.at[k, sample_rows(space_at(d)), :],
                noise.at[k, :, cols(sp)],
                (space_at(d), me),
            )
            for d in range(1, n_space)
        ]

    def send_sums(k, c, i=None):
        alpha = constants(k)[1]
        some = pl.ds(0, members) if i is None else group_at(i)
        parts = [xt[j, :, some] for j in range(PARTS)]
        inner = product(z[chunk_rows(c), :], parts, 0)
        gram[k, c, :, some] = 2.0 * alpha * inner - alpha * alpha * norms[:, some]
        for d in range(1, n_mem):
            rows_to = rows_at(pair(d) * own_rows, own_rows) if scatter else pl.ds(0, rows)
            inbound["sums", k, c].append(
                put(
                    ("sums", c, i or 0, d),
                    gram.at[k, c, rows_to, some],
                    sums.at[k, c, d - 1, :, some],
                    (sp, pair(d)),
                )
            )

    def send_weights(k, c):
        total = gram[k, c, owned(), :]
        for copy in inbound["sums", k, c]:
            copy.wait_recv()
        for d in range(n_mem - 1):
            total = total + sums[k, c, d]
        logits = total / (2.0 * constants(k)[0] * temper)
        e = jnp.exp(logits - jnp.max(logits, axis=1, keepdims=True))
        w[k, c, owned(), :] = e / jnp.sum(e, axis=1, keepdims=True)
        inbound["give", k, c] = []
        if scatter:
            at = w.at[k, c, owned(), :]
            inbound["give", k, c] = [
                put(("give", c, d) if c else ("mem", d), at, at, (sp, pair(d)))
                for d in range(1, n_mem)
            ]

    def advance(k, c):
        t, alpha, drift, g2, damp = constants(k)
        zs = z[chunk_rows(c), :]
        seen_term = damp * 4.0 * (seen[...] - arctan(zs)) / (1.0 + zs * zs)
        z[chunk_rows(c), :] = (
            zs
            + dt * (-drift * zs + g2 * (seen_term - zs / t))
            + math.sqrt(dt * g2) * noise[k, chunk_rows(c), :]
        )

    def add_blend(k, c):
        t, alpha, _, g2, _ = constants(k)
        for copy in inbound["give", k, c]:
            copy.wait_recv()
        blend = product(w[k, c], [xb[j] for j in range(PARTS)], 0)
        z[chunk_rows(c), :] = z[chunk_rows(c), :] + (dt * g2 * alpha / t) * blend

    each = list(range(chunks))
    results = []
    arriving = {}
    for k in range(ITERS):
        for c in each:
            inbound["sums", k, c] = []
    for copy in starts[0]:
        copy.wait_recv()

    def finish_group(i):
        for copy in onward[i]:
            copy.wait_recv()
        for d in range(1, nx):
            take(lax.rem(xi + d, nx) * CORES + 1 - core, i)
        send_sums(0, 0, i)

    for i in groups:
        pass_core(i)
        for d in range(1, nx):
            take(x_at(d), i)
        to_core[i].wait_recv()
        take(xi * CORES + 1 - core, i)
        if i:
            finish_group(i - 1)
    finish_group(len(groups) - 1)
    for k in range(ITERS):
        for c in each:
            if k > 0:
                add_blend(k - 1, c)
            elif c > 0:
                for copy in starts[c]:
                    copy.wait_recv()
            if k + c > 0:
                send_sums(k, c)
        if k == 0:
            arriving[0] = send_noise(0)
        for c in each:
            send_weights(k, c)
        if k + 1 < ITERS:
            arriving[k + 1] = send_noise(k + 1)
        if k == 0:
            loads[3].wait()
            for copy in firsts:
                copy.wait_recv()
        for copy in arriving[k]:
            copy.wait_recv()
        for c in each:
            advance(k, c)
    for c in each:
        add_blend(ITERS - 1, c)
        target = out.at[rows_at(sp * samples + c * rows, rows), :]
        results += [
            put(("space", c, d), z.at[chunk_rows(c), cols(space_at(d))], target, (space_at(d), me))
            for d in range(1, n_space)
        ]
        own = pltpu.make_async_copy(z.at[chunk_rows(c), cols(sp)], target, local.at[4 + c])
        own.start()
        loads.append(own)
    for copy in loads[4:]:
        copy.wait()
    for copy in results:
        copy.wait_recv()
    for copy in pending.values():
        copy.wait_send()


def per_device(prior, terminal, perturbation, angles):
    n_space, n_mem = lax.axis_size("space"), lax.axis_size("mem")
    all_samples, variables = terminal.shape
    members = prior.shape[0] * n_mem
    samples = all_samples // n_space
    chunks = CHUNKS
    while chunks > 1 and samples % (chunks * n_mem * SUBLANES):
        chunks //= 2
    rows = samples // chunks
    scatter = rows % (n_mem * SUBLANES) == 0
    own_rows = rows // n_mem if scatter else rows
    block = prior.shape[0]
    groups = n_mem // max(1, LANES // block)
    wide = n_space * variables
    assert n_mem & (n_mem - 1) == 0
    temper = math.sqrt(wide * n_mem)
    f32 = jnp.float32
    nx = n_space // CORES
    iters = perturbation.shape[0]
    steps = (groups + 2 * chunks - 1) * (n_mem - 1)
    slots = steps + (chunks + 1 + iters) * (n_space - 1) + n_mem * (nx - 1) + groups * nx
    operands = prior, terminal, perturbation, angles.reshape(1, variables)
    anywhere = pl.BlockSpec(memory_space=pl.ANY)
    return pl.pallas_call(
        functools.partial(kernel, (n_space, n_mem, scatter, temper)),
        out_shape=jax.ShapeDtypeStruct((all_samples, variables), f32),
        in_specs=[anywhere] * 4,
        out_specs=anywhere,
        scratch_shapes=[
            pltpu.VMEM((n_space, members, variables), f32),
            pltpu.VMEM((samples, wide), f32),
            pltpu.VMEM((iters, samples, wide), f32),
            pltpu.VMEM((1, wide), f32),
            pltpu.VMEM((iters, chunks, rows, members), f32),
            pltpu.VMEM((iters, chunks, n_mem - 1, own_rows, members), f32),
            pltpu.VMEM((iters, chunks, rows, members), f32),
            pltpu.VMEM((PARTS, members, wide), jnp.bfloat16),
            pltpu.VMEM((PARTS, wide, members), jnp.bfloat16),
            pltpu.VMEM((1, members), f32),
            pltpu.SemaphoreType.DMA((slots,)),
            pltpu.SemaphoreType.DMA((slots,)),
            pltpu.SemaphoreType.DMA((4 + chunks,)),
        ],
        compiler_params=pltpu.CompilerParams(
            collective_id=0, has_side_effects=True, vmem_limit_bytes=VMEM_LIMIT
        ),
    )(*[pltpu.with_memory_space_constraint(a, pltpu.HBM) for a in operands])


def solution(mesh):
    in_specs = (
        P("mem", "space"),
        P(None, ("space", "mem")),
        P(None, None, ("space", "mem")),
        P(("space", "mem")),
    )
    out_specs = P(None, ("space", "mem"))
    return jax.shard_map(
        per_device, mesh=mesh, in_specs=in_specs, out_specs=out_specs, check_vma=False
    )
```

```python
import functools
import math

import jax
import jax.numpy as jnp
from jax import lax
from jax.experimental import pallas as pl
from jax.experimental.pallas import tpu as pltpu
from jax.sharding import PartitionSpec as P

ITERS = 3
CHUNKS = 2
PIECE = 8
PARTS = 2
VMEM_LIMIT = 48 << 20
CORES = 2
SUBLANES = 8
LANES = 128
MESH = pl.DeviceIdType.MESH


def split(a, parts):
    out = []
    for _ in range(parts):
        out.append(a.astype(jnp.bfloat16))
        a = a - out[-1].astype(jnp.float32)
    return out


def product(a, parts, contract_b):
    n = a.shape[0]
    lhs = split(a, len(parts))
    total = None
    for i in reversed(range(len(parts))):
        rows = lhs[: len(parts) - i]
        both = lax.dot_general(
            jnp.concatenate(rows, axis=0),
            parts[i],
            (((1,), (contract_b,)), ((), ())),
            preferred_element_type=jnp.float32,
        )
        for j in reversed(range(len(rows))):
            term = both[j * n : (j + 1) * n]
            total = term if total is None else total + term
    return total


def arctan(x):
    a = jnp.abs(x)
    big = a > 2.414213562373095
    mid = a > 0.4142135623730950
    num = jnp.where(big, -1.0, jnp.where(mid, a - 1.0, a))
    den = jnp.where(big, a, jnp.where(mid, a + 1.0, 1.0))
    base = jnp.where(big, math.pi / 2, jnp.where(mid, math.pi / 4, 0.0))
    r = num / den
    s = r * r
    poly = ((8.05374449538e-2 * s - 1.38776856032e-1) * s + 1.99777106478e-1) * s
    poly = (poly - 3.33329491539e-1) * s * r + r
    y = base + poly
    return jnp.where(x < 0.0, -y, y)


def rows_at(start, size):
    return pl.ds(pl.multiple_of(start, SUBLANES), size)


def constants(k):
    t = 1.0 - k / ITERS
    alpha = 1.0 - 0.5 * t
    return t, alpha, -0.5 / alpha, 1.0 + t / alpha, 1.0 - t


def kernel(
    plan,
    prior,
    terminal,
    perturbation,
    angles,
    out,
    x,
    z,
    noise,
    seen,
    gram,
    sums,
    w,
    xb,
    xt,
    norms,
    send,
    recv,
    local,
):
    n_space, n_mem, scatter, temper = plan
    _, chunks, pieces, own_rows, members = gram.shape
    rows = pieces * own_rows
    samples = z.shape[0]
    block = prior.shape[0]
    variables = terminal.shape[1]
    nx = n_space // CORES
    dt = 1.0 / ITERS

    sp = lax.axis_index("space")
    me = lax.axis_index("mem")
    core = lax.rem(sp, CORES)
    xi = lax.div(sp, CORES)
    partner = (xi * CORES + 1 - core, me)

    def space_at(d):
        return lax.rem(sp + d + n_space, n_space)

    def x_at(d):
        return lax.rem(xi + d + nx, nx) * CORES + core

    def pair(d):
        p = me
        bit = 1
        while bit < n_mem:
            if d & bit:
                p = p + bit - 2 * bit * lax.rem(lax.div(me, bit), 2)
            bit *= 2
        return p

    def cols(p):
        return pl.ds(pl.multiple_of(p * variables, variables), variables)

    def block_rows(p):
        return rows_at(p * block, block)

    def chunk_rows(c):
        return pl.ds(c * rows, rows)

    def sample_rows(p):
        return rows_at(p * samples, samples)

    loads = [
        pltpu.make_async_copy(prior.at[:, cols(me)], x.at[sp, block_rows(me), :], local.at[0]),
        pltpu.make_async_copy(terminal.at[sample_rows(sp), :], z.at[:, cols(sp)], local.at[1]),
        pltpu.make_async_copy(angles, seen.at[:, cols(sp)], local.at[2]),
        pltpu.make_async_copy(
            perturbation.at[:, sample_rows(sp), :], noise.at[:, :, cols(sp)], local.at[3]
        ),
    ]
    for copy in loads:
        copy.start()

    barrier = pltpu.get_barrier_semaphore()
    greet = [(space_at(d), me) for d in range(1, n_space)]
    greet += [(sp, pair(d)) for d in range(1, n_mem)]
    for dev in greet:
        pl.semaphore_signal(barrier, inc=1, device_id=dev, device_id_type=MESH)
    pl.semaphore_wait(barrier, len(greet))

    together = max(1, LANES // block)
    groups = range(n_mem // together)
    slots = {}
    pending = {}

    def copy_at(key, src, dst, dev):
        i = slots.setdefault(key, len(slots))
        return pltpu.make_async_remote_copy(
            src_ref=src,
            dst_ref=dst,
            send_sem=send.at[i],
            recv_sem=recv.at[i],
            device_id=dev,
            device_id_type=MESH,
        )

    def put(key, src, dst, dev):
        return put_all(key, [(src, dst, dev)], dst)

    def put_all(key, copies, landing):
        if key in pending:
            pending[key].wait_send()
        for src, dst, dev in copies:
            copy_at(key, src, dst, dev).start()
        pending[key] = copy_at(key, landing, landing, copies[0][2])
        return pending[key]

    here = x.at[sp, block_rows(me), :]
    others = pl.ds(0, (n_space - 1) * variables)
    exchange = {
        d: put(("mem", d), prior.at[:, cols(pair(d))], here, (sp, pair(d)))
        for d in range(1, n_mem)
    }

    def send_start(c):
        copies = []
        for d in range(1, n_space):
            q = space_at(d)
            src = terminal.at[rows_at(q * samples + c * rows, rows), :]
            copies.append((src, z.at[chunk_rows(c), cols(sp)], (q, me)))
        return put_all(("space", c), copies, z.at[chunk_rows(c), others])

    starts = [send_start(0)]

    over_x, to_core, onward = [], [], []

    def group_at(i):
        return rows_at(lax.div(pair(i * together), together) * together * block, together * block)

    def group_blocks(i):
        return range(i * together, (i + 1) * together)

    def pass_on(b, src, at):
        over_x.append(
            [put(("x", b, d), src, at, (x_at(d), me)) for d in range(1, nx)]
        )

    def pass_core(i):
        for b in group_blocks(i):
            for copy in over_x[b]:
                copy.wait_recv()
        onward.append([])
        for d in range(1, nx):
            at = x.at[x_at(-d), group_at(i), :]
            onward[i].append(put(("onward", i, d), at, at, partner))

    def take(q, i):
        some = group_at(i)
        xs = x[q, some, :]
        for j, piece in enumerate(split(xs, PARTS)):
            xb[j, some, cols(q)] = piece
        turned = xs.T
        for j, piece in enumerate(split(turned, PARTS)):
            xt[j, cols(q), some] = piece
        norms[:, some] = norms[:, some] + jnp.sum(turned * turned, axis=0, keepdims=True)

    norms[...] = jnp.zeros_like(norms)
    pass_on(0, prior.at[:, cols(me)], here)
    loads[0].wait()
    for i in groups:
        for d in group_blocks(i):
            if d:
                exchange[d].wait_recv()
                at = x.at[sp, block_rows(pair(d)), :]
                pass_on(d, at, at)
        at = x.at[sp, group_at(i), :]
        to_core.append(put(("core", i), at, at, partner))
        take(sp, i)
    starts += [send_start(c) for c in range(1, chunks)]
    firsts = put_all(
        "angles",
        [(angles, seen.at[:, cols(sp)], (space_at(d), me)) for d in range(1, n_space)],
        seen.at[:, others],
    )
    for copy in loads[1:3]:
        copy.wait()

    inbound = {}

    owned = me if scatter else 0

    def send_noise(k):
        copies = []
        for d in range(1, n_space):
            q = space_at(d)
            src = perturbation.at[k, sample_rows(q), :]
            copies.append((src, noise.at[k, :, cols(sp)], (q, me)))
        return put_all(("noise", k), copies, noise.at[k, :, others])

    def send_sums(k, c, i=None):
        alpha = constants(k)[1]
        some = pl.ds(0, members) if i is None else group_at(i)
        parts = [xt[j, :, some] for j in range(PARTS)]
        inner = product(z[chunk_rows(c), :], parts, 0)
        value = 2.0 * alpha * inner - alpha * alpha * norms[:, some]
        gram[k, c, :, :, some] = value.reshape(pieces, own_rows, value.shape[1])
        copies = []
        for d in range(1, n_mem):
            src = gram.at[k, c, pair(d) if scatter else 0, :, some]
            copies.append((src, sums.at[k, c, d - 1, :, some], (sp, pair(d))))
        landing = sums.at[k, c, :, :, some]
        inbound["sums", k, c].append(put_all(("sums", c, i or 0), copies, landing))

    def send_weights(k, c):
        total = gram[k, c, owned]
        for copy in inbound["sums", k, c]:
            copy.wait_recv()
        for d in range(n_mem - 1):
            total = total + sums[k, c, d]
        logits = total / (2.0 * constants(k)[0] * temper)
        e = jnp.exp(logits - jnp.max(logits, axis=1, keepdims=True))
        w[k, c, owned] = e / jnp.sum(e, axis=1, keepdims=True)
        if scatter:
            at = w.at[k, c, owned]
            copies = [(at, at, (sp, pair(d))) for d in range(1, n_mem)]
            landing = w.at[k, c, pl.ds(0, n_mem - 1)]
            inbound["give", k, c] = put_all(("give", c), copies, landing)

    def advance(k, c):
        t, alpha, drift, g2, damp = constants(k)
        zs = z[chunk_rows(c), :]
        seen_term = damp * 4.0 * (seen[...] - arctan(zs)) / (1.0 + zs * zs)
        z[chunk_rows(c), :] = (
            zs
            + dt * (-drift * zs + g2 * (seen_term - zs / t))
            + math.sqrt(dt * g2) * noise[k, chunk_rows(c), :]
        )

    def add_blend(k, c):
        t, alpha, _, g2, _ = constants(k)
        if scatter:
            inbound["give", k, c].wait_recv()
        blend = product(w[k, c].reshape(rows, members), [xb[j] for j in range(PARTS)], 0)
        z[chunk_rows(c), :] = z[chunk_rows(c), :] + (dt * g2 * alpha / t) * blend

    each = list(range(chunks))
    results = []
    arriving = {}
    for k in range(ITERS):
        for c in each:
            inbound["sums", k, c] = []
    starts[0].wait_recv()

    def finish_group(i):
        for copy in onward[i]:
            copy.wait_recv()
        for d in range(1, nx):
            take(lax.rem(xi + d, nx) * CORES + 1 - core, i)
        send_sums(0, 0, i)

    for i in groups:
        pass_core(i)
        for d in range(1, nx):
            take(x_at(d), i)
        to_core[i].wait_recv()
        take(xi * CORES + 1 - core, i)
        if i:
            finish_group(i - 1)
    finish_group(len(groups) - 1)
    for k in range(ITERS):
        for c in each:
            if k > 0:
                add_blend(k - 1, c)
            elif c > 0:
                starts[c].wait_recv()
            if k + c > 0:
                send_sums(k, c)
        if k == 0:
            arriving[0] = send_noise(0)
        for c in each:
            send_weights(k, c)
        if k + 1 < ITERS:
            arriving[k + 1] = send_noise(k + 1)
        if k == 0:
            loads[3].wait()
            firsts.wait_recv()
        arriving[k].wait_recv()
        for c in each:
            advance(k, c)
    for c in each:
        add_blend(ITERS - 1, c)
        target = out.at[rows_at(sp * samples + c * rows, rows), :]
        copies = []
        for d in range(1, n_space):
            q = space_at(d)
            copies.append((z.at[chunk_rows(c), cols(q)], target, (q, me)))
        results.append(put_all(("space", c), copies, z.at[chunk_rows(c), others]))
        own = pltpu.make_async_copy(z.at[chunk_rows(c), cols(sp)], target, local.at[4 + c])
        own.start()
        loads.append(own)
    for copy in loads[4:]:
        copy.wait()
    for copy in results:
        copy.wait_recv()
    for copy in pending.values():
        copy.wait_send()


def per_device(prior, terminal, perturbation, angles):
    n_space, n_mem = lax.axis_size("space"), lax.axis_size("mem")
    all_samples, variables = terminal.shape
    members = prior.shape[0] * n_mem
    samples = all_samples // n_space
    chunks = CHUNKS
    while chunks > 1 and samples % (chunks * n_mem * PIECE):
        chunks //= 2
    rows = samples // chunks
    scatter = rows % (n_mem * PIECE) == 0
    pieces = n_mem if scatter else 1
    own_rows = rows // pieces
    block = prior.shape[0]
    groups = n_mem // max(1, LANES // block)
    wide = n_space * variables
    assert n_mem & (n_mem - 1) == 0
    temper = math.sqrt(wide * n_mem)
    f32 = jnp.float32
    nx = n_space // CORES
    iters = perturbation.shape[0]
    slots = n_mem - 1 + n_mem * (nx - 1) + groups * (nx + 1) + 3 * chunks + iters
    operands = prior, terminal, perturbation, angles.reshape(1, variables)
    anywhere = pl.BlockSpec(memory_space=pl.ANY)
    return pl.pallas_call(
        functools.partial(kernel, (n_space, n_mem, scatter, temper)),
        out_shape=jax.ShapeDtypeStruct((all_samples, variables), f32),
        in_specs=[anywhere] * 4,
        out_specs=anywhere,
        scratch_shapes=[
            pltpu.VMEM((n_space, members, variables), f32),
            pltpu.VMEM((samples, wide), f32),
            pltpu.VMEM((iters, samples, wide), f32),
            pltpu.VMEM((1, wide), f32),
            pltpu.VMEM((iters, chunks, pieces, own_rows, members), f32),
            pltpu.VMEM((iters, chunks, n_mem - 1, own_rows, members), f32),
            pltpu.VMEM((iters, chunks, pieces, own_rows, members), f32),
            pltpu.VMEM((PARTS, members, wide), jnp.bfloat16),
            pltpu.VMEM((PARTS, wide, members), jnp.bfloat16),
            pltpu.VMEM((1, members), f32),
            pltpu.SemaphoreType.DMA((slots,)),
            pltpu.SemaphoreType.DMA((slots,)),
            pltpu.SemaphoreType.DMA((4 + chunks,)),
        ],
        compiler_params=pltpu.CompilerParams(
            collective_id=0, has_side_effects=True, vmem_limit_bytes=VMEM_LIMIT
        ),
    )(*[pltpu.with_memory_space_constraint(a, pltpu.HBM) for a in operands])


def solution(mesh):
    in_specs = (
        P("mem", "space"),
        P(None, ("space", "mem")),
        P(None, None, ("space", "mem")),
        P(("space", "mem")),
    )
    out_specs = P(None, ("space", "mem"))
    return jax.shard_map(
        per_device, mesh=mesh, in_specs=in_specs, out_specs=out_specs, check_vma=False
    )
```

```python
import functools
import math

import jax
import jax.numpy as jnp
from jax import lax
from jax.experimental import pallas as pl
from jax.experimental.pallas import tpu as pltpu
from jax.sharding import PartitionSpec as P

ITERS = 3
CHUNKS = 2
PIECE = 8
PARTS = 2
VMEM_LIMIT = 48 << 20
CORES = 2
SUBLANES = 8
LANES = 128
MESH = pl.DeviceIdType.MESH


def split(a, parts):
    out = []
    for _ in range(parts):
        out.append(a.astype(jnp.bfloat16))
        a = a - out[-1].astype(jnp.float32)
    return out


def product(a, parts, contract_b):
    n = a.shape[0]
    lhs = split(a, len(parts))
    total = None
    for i in reversed(range(len(parts))):
        rows = lhs[: len(parts) - i]
        both = lax.dot_general(
            jnp.concatenate(rows, axis=0),
            parts[i],
            (((1,), (contract_b,)), ((), ())),
            preferred_element_type=jnp.float32,
        )
        for j in reversed(range(len(rows))):
            term = both[j * n : (j + 1) * n]
            total = term if total is None else total + term
    return total


def arctan(x):
    a = jnp.abs(x)
    big = a > 2.414213562373095
    mid = a > 0.4142135623730950
    num = jnp.where(big, -1.0, jnp.where(mid, a - 1.0, a))
    den = jnp.where(big, a, jnp.where(mid, a + 1.0, 1.0))
    base = jnp.where(big, math.pi / 2, jnp.where(mid, math.pi / 4, 0.0))
    r = num / den
    s = r * r
    poly = ((8.05374449538e-2 * s - 1.38776856032e-1) * s + 1.99777106478e-1) * s
    poly = (poly - 3.33329491539e-1) * s * r + r
    y = base + poly
    return jnp.where(x < 0.0, -y, y)


def rows_at(start, size):
    return pl.ds(pl.multiple_of(start, SUBLANES), size)


def constants(k):
    t = 1.0 - k / ITERS
    alpha = 1.0 - 0.5 * t
    return t, alpha, -0.5 / alpha, 1.0 + t / alpha, 1.0 - t


def kernel(
    plan,
    prior,
    terminal,
    perturbation,
    angles,
    out,
    x,
    z,
    noise,
    seen,
    gram,
    sums,
    w,
    xb,
    xt,
    norms,
    send,
    recv,
    local,
):
    n_space, n_mem, scatter, temper = plan
    _, chunks, pieces, own_rows, members = gram.shape
    rows = pieces * own_rows
    samples = z.shape[0]
    block = prior.shape[0]
    variables = terminal.shape[1]
    nx = n_space // CORES
    dt = 1.0 / ITERS

    sp = lax.axis_index("space")
    me = lax.axis_index("mem")
    core = lax.rem(sp, CORES)
    xi = lax.div(sp, CORES)
    partner = (xi * CORES + 1 - core, me)

    def space_at(d):
        return lax.rem(sp + d + n_space, n_space)

    def x_at(d):
        return lax.rem(xi + d + nx, nx) * CORES + core

    def pair(d):
        p = me
        bit = 1
        while bit < n_mem:
            if d & bit:
                p = p + bit - 2 * bit * lax.rem(lax.div(me, bit), 2)
            bit *= 2
        return p

    def cols(p):
        return pl.ds(pl.multiple_of(p * variables, variables), variables)

    def block_rows(p):
        return rows_at(p * block, block)

    def chunk_rows(c):
        return pl.ds(c * rows, rows)

    def sample_rows(p):
        return rows_at(p * samples, samples)

    loads = [
        pltpu.make_async_copy(prior.at[:, cols(me)], x.at[sp, block_rows(me), :], local.at[0]),
        pltpu.make_async_copy(terminal.at[sample_rows(sp), :], z.at[:, cols(sp)], local.at[1]),
        pltpu.make_async_copy(angles, seen.at[:, cols(sp)], local.at[2]),
        pltpu.make_async_copy(
            perturbation.at[:, sample_rows(sp), :], noise.at[:, :, cols(sp)], local.at[3]
        ),
    ]
    for copy in loads:
        copy.start()

    barrier = pltpu.get_barrier_semaphore()
    greet = [(space_at(d), me) for d in range(1, n_space)]
    greet += [(sp, pair(d)) for d in range(1, n_mem)]
    for dev in greet:
        pl.semaphore_signal(barrier, inc=1, device_id=dev, device_id_type=MESH)
    pl.semaphore_wait(barrier, len(greet))

    together = max(1, LANES // block)
    groups = range(n_mem // together)
    slots = {}
    pending = {}

    def copy_at(key, src, dst, dev):
        i = slots.setdefault(key, len(slots))
        return pltpu.make_async_remote_copy(
            src_ref=src,
            dst_ref=dst,
            send_sem=send.at[i],
            recv_sem=recv.at[i],
            device_id=dev,
            device_id_type=MESH,
        )

    def put(key, src, dst, dev):
        return put_all(key, [(src, dst, dev)], dst)

    def put_all(key, copies, landing):
        if key in pending:
            pending[key].wait_send()
        for src, dst, dev in copies:
            copy_at(key, src, dst, dev).start()
        pending[key] = copy_at(key, landing, landing, copies[0][2])
        return pending[key]

    here = x.at[sp, block_rows(me), :]
    others = pl.ds(0, (n_space - 1) * variables)
    exchange = {
        d: put(("mem", d), prior.at[:, cols(pair(d))], here, (sp, pair(d)))
        for d in range(1, n_mem)
    }

    def send_start(c):
        copies = []
        for d in range(1, n_space):
            q = space_at(d)
            src = terminal.at[rows_at(q * samples + c * rows, rows), :]
            copies.append((src, z.at[chunk_rows(c), cols(sp)], (q, me)))
        return put_all(("space", c), copies, z.at[chunk_rows(c), others])

    starts = [send_start(0)]

    over_x, to_core, onward = [], [], []

    def group_at(i):
        return rows_at(lax.div(pair(i * together), together) * together * block, together * block)

    def group_blocks(i):
        return range(i * together, (i + 1) * together)

    def pass_on(b, src, at):
        over_x.append(
            [put(("x", b, d), src, at, (x_at(d), me)) for d in range(1, nx)]
        )

    def pass_core(i):
        for b in group_blocks(i):
            for copy in over_x[b]:
                copy.wait_recv()
        onward.append([])
        for d in range(1, nx):
            at = x.at[x_at(-d), group_at(i), :]
            onward[i].append(put(("onward", i, d), at, at, partner))

    def take(q, i):
        some = group_at(i)
        xs = x[q, some, :]
        for j, piece in enumerate(split(xs, PARTS)):
            xb[j, some, cols(q)] = piece
        turned = xs.T
        for j, piece in enumerate(split(turned, PARTS)):
            xt[j, cols(q), some] = piece
        norms[:, some] = norms[:, some] + jnp.sum(turned * turned, axis=0, keepdims=True)

    norms[...] = jnp.zeros_like(norms)
    pass_on(0, prior.at[:, cols(me)], here)
    loads[0].wait()
    for i in groups:
        for d in group_blocks(i):
            if d:
                exchange[d].wait_recv()
                at = x.at[sp, block_rows(pair(d)), :]
                pass_on(d, at, at)
        at = x.at[sp, group_at(i), :]
        to_core.append(put(("core", i), at, at, partner))
        take(sp, i)
    starts += [send_start(c) for c in range(1, chunks)]
    firsts = put_all(
        "angles",
        [(angles, seen.at[:, cols(sp)], (space_at(d), me)) for d in range(1, n_space)],
        seen.at[:, others],
    )
    for copy in loads[1:3]:
        copy.wait()

    inbound = {}

    owned = me if scatter else 0

    def send_noise(k):
        copies = []
        for d in range(1, n_space):
            q = space_at(d)
            src = perturbation.at[k, sample_rows(q), :]
            copies.append((src, noise.at[k, :, cols(sp)], (q, me)))
        return put_all(("noise", k), copies, noise.at[k, :, others])

    def send_sums(k, c, i=None):
        alpha = constants(k)[1]
        some = pl.ds(0, members) if i is None else group_at(i)
        parts = [xt[j, :, some] for j in range(PARTS)]
        inner = product(z[chunk_rows(c), :], parts, 0)
        value = 2.0 * alpha * inner - alpha * alpha * norms[:, some]
        gram[k, c, :, :, some] = value.reshape(pieces, own_rows, value.shape[1])
        copies = []
        for d in reversed(range(1, n_mem)):
            src = gram.at[k, c, pair(d) if scatter else 0, :, some]
            copies.append((src, sums.at[k, c, d - 1, :, some], (sp, pair(d))))
        landing = sums.at[k, c, :, :, some]
        inbound["sums", k, c].append(put_all(("sums", c, i or 0), copies, landing))

    def send_weights(k, c):
        total = gram[k, c, owned]
        for copy in inbound["sums", k, c]:
            copy.wait_recv()
        for d in range(n_mem - 1):
            total = total + sums[k, c, d]
        logits = total / (2.0 * constants(k)[0] * temper)
        e = jnp.exp(logits - jnp.max(logits, axis=1, keepdims=True))
        w[k, c, owned] = e / jnp.sum(e, axis=1, keepdims=True)
        if scatter:
            at = w.at[k, c, owned]
            copies = [(at, at, (sp, pair(d))) for d in reversed(range(1, n_mem))]
            landing = w.at[k, c, pl.ds(0, n_mem - 1)]
            inbound["give", k, c] = put_all(("give", c), copies, landing)

    def advance(k, c):
        t, alpha, drift, g2, damp = constants(k)
        zs = z[chunk_rows(c), :]
        seen_term = damp * 4.0 * (seen[...] - arctan(zs)) / (1.0 + zs * zs)
        z[chunk_rows(c), :] = (
            zs
            + dt * (-drift * zs + g2 * (seen_term - zs / t))
            + math.sqrt(dt * g2) * noise[k, chunk_rows(c), :]
        )

    def add_blend(k, c):
        t, alpha, _, g2, _ = constants(k)
        if scatter:
            inbound["give", k, c].wait_recv()
        blend = product(w[k, c].reshape(rows, members), [xb[j] for j in range(PARTS)], 0)
        z[chunk_rows(c), :] = z[chunk_rows(c), :] + (dt * g2 * alpha / t) * blend

    each = list(range(chunks))
    results = []
    arriving = {}
    for k in range(ITERS):
        for c in each:
            inbound["sums", k, c] = []
    starts[0].wait_recv()

    def finish_group(i):
        for copy in onward[i]:
            copy.wait_recv()
        for d in range(1, nx):
            take(lax.rem(xi + d, nx) * CORES + 1 - core, i)
        send_sums(0, 0, i)

    for i in groups:
        pass_core(i)
        for d in range(1, nx):
            take(x_at(d), i)
        to_core[i].wait_recv()
        take(xi * CORES + 1 - core, i)
        if i:
            finish_group(i - 1)
    finish_group(len(groups) - 1)
    for k in range(ITERS):
        for c in each:
            if k > 0:
                add_blend(k - 1, c)
            elif c > 0:
                starts[c].wait_recv()
            if k + c > 0:
                send_sums(k, c)
        if k == 0:
            arriving[0] = send_noise(0)
        for c in each:
            send_weights(k, c)
        if k + 1 < ITERS:
            arriving[k + 1] = send_noise(k + 1)
        if k == 0:
            loads[3].wait()
            firsts.wait_recv()
        arriving[k].wait_recv()
        for c in each:
            advance(k, c)
    for c in each:
        add_blend(ITERS - 1, c)
        target = out.at[rows_at(sp * samples + c * rows, rows), :]
        copies = []
        for d in range(1, n_space):
            q = space_at(d)
            copies.append((z.at[chunk_rows(c), cols(q)], target, (q, me)))
        results.append(put_all(("space", c), copies, z.at[chunk_rows(c), others]))
        own = pltpu.make_async_copy(z.at[chunk_rows(c), cols(sp)], target, local.at[4 + c])
        own.start()
        loads.append(own)
    for copy in loads[4:]:
        copy.wait()
    for copy in results:
        copy.wait_recv()
    for copy in pending.values():
        copy.wait_send()


def per_device(prior, terminal, perturbation, angles):
    n_space, n_mem = lax.axis_size("space"), lax.axis_size("mem")
    all_samples, variables = terminal.shape
    members = prior.shape[0] * n_mem
    samples = all_samples // n_space
    chunks = CHUNKS
    while chunks > 1 and samples % (chunks * n_mem * PIECE):
        chunks //= 2
    rows = samples // chunks
    scatter = rows % (n_mem * PIECE) == 0
    pieces = n_mem if scatter else 1
    own_rows = rows // pieces
    block = prior.shape[0]
    groups = n_mem // max(1, LANES // block)
    wide = n_space * variables
    assert n_mem & (n_mem - 1) == 0
    temper = math.sqrt(wide * n_mem)
    f32 = jnp.float32
    nx = n_space // CORES
    iters = perturbation.shape[0]
    slots = n_mem - 1 + n_mem * (nx - 1) + groups * (nx + 1) + 3 * chunks + iters
    operands = prior, terminal, perturbation, angles.reshape(1, variables)
    anywhere = pl.BlockSpec(memory_space=pl.ANY)
    return pl.pallas_call(
        functools.partial(kernel, (n_space, n_mem, scatter, temper)),
        out_shape=jax.ShapeDtypeStruct((all_samples, variables), f32),
        in_specs=[anywhere] * 4,
        out_specs=anywhere,
        scratch_shapes=[
            pltpu.VMEM((n_space, members, variables), f32),
            pltpu.VMEM((samples, wide), f32),
            pltpu.VMEM((iters, samples, wide), f32),
            pltpu.VMEM((1, wide), f32),
            pltpu.VMEM((iters, chunks, pieces, own_rows, members), f32),
            pltpu.VMEM((iters, chunks, n_mem - 1, own_rows, members), f32),
            pltpu.VMEM((iters, chunks, pieces, own_rows, members), f32),
            pltpu.VMEM((PARTS, members, wide), jnp.bfloat16),
            pltpu.VMEM((PARTS, wide, members), jnp.bfloat16),
            pltpu.VMEM((1, members), f32),
            pltpu.SemaphoreType.DMA((slots,)),
            pltpu.SemaphoreType.DMA((slots,)),
            pltpu.SemaphoreType.DMA((4 + chunks,)),
        ],
        compiler_params=pltpu.CompilerParams(
            collective_id=0, has_side_effects=True, vmem_limit_bytes=VMEM_LIMIT
        ),
    )(*[pltpu.with_memory_space_constraint(a, pltpu.HBM) for a in operands])


def solution(mesh):
    in_specs = (
        P("mem", "space"),
        P(None, ("space", "mem")),
        P(None, None, ("space", "mem")),
        P(("space", "mem")),
    )
    out_specs = P(None, ("space", "mem"))
    return jax.shard_map(
        per_device, mesh=mesh, in_specs=in_specs, out_specs=out_specs, check_vma=False
    )
```

```python
import functools
import math

import jax
import jax.numpy as jnp
from jax import lax
from jax.experimental import pallas as pl
from jax.experimental.pallas import tpu as pltpu
from jax.sharding import PartitionSpec as P

ITERS = 3
CHUNKS = 2
PIECE = 8
PARTS = 2
VMEM_LIMIT = 48 << 20
CORES = 2
SUBLANES = 8
LANES = 128
MESH = pl.DeviceIdType.MESH


def split(a, parts):
    out = []
    for _ in range(parts):
        out.append(a.astype(jnp.bfloat16))
        a = a - out[-1].astype(jnp.float32)
    return out


def product(a, parts, contract_b):
    n = a.shape[0]
    lhs = split(a, len(parts))
    total = None
    for i in reversed(range(len(parts))):
        rows = lhs[: len(parts) - i]
        both = lax.dot_general(
            jnp.concatenate(rows, axis=0),
            parts[i],
            (((1,), (contract_b,)), ((), ())),
            preferred_element_type=jnp.float32,
        )
        for j in reversed(range(len(rows))):
            term = both[j * n : (j + 1) * n]
            total = term if total is None else total + term
    return total


def arctan(x):
    a = jnp.abs(x)
    big = a > 2.414213562373095
    mid = a > 0.4142135623730950
    num = jnp.where(big, -1.0, jnp.where(mid, a - 1.0, a))
    den = jnp.where(big, a, jnp.where(mid, a + 1.0, 1.0))
    base = jnp.where(big, math.pi / 2, jnp.where(mid, math.pi / 4, 0.0))
    r = num / den
    s = r * r
    poly = ((8.05374449538e-2 * s - 1.38776856032e-1) * s + 1.99777106478e-1) * s
    poly = (poly - 3.33329491539e-1) * s * r + r
    y = base + poly
    return jnp.where(x < 0.0, -y, y)


def rows_at(start, size):
    return pl.ds(pl.multiple_of(start, SUBLANES), size)


def constants(k):
    t = 1.0 - k / ITERS
    alpha = 1.0 - 0.5 * t
    return t, alpha, -0.5 / alpha, 1.0 + t / alpha, 1.0 - t


def kernel(
    plan,
    prior,
    terminal,
    perturbation,
    angles,
    out,
    x,
    z,
    noise,
    seen,
    gram,
    sums,
    w,
    xb,
    xt,
    norms,
    send,
    recv,
    local,
):
    n_space, n_mem, scatter, temper = plan
    _, chunks, pieces, own_rows, members = gram.shape
    rows = pieces * own_rows
    samples = z.shape[0]
    block = prior.shape[0]
    variables = terminal.shape[1]
    nx = n_space // CORES
    dt = 1.0 / ITERS

    sp = lax.axis_index("space")
    me = lax.axis_index("mem")
    core = lax.rem(sp, CORES)
    xi = lax.div(sp, CORES)
    partner = (xi * CORES + 1 - core, me)

    def space_at(d):
        over, flip = divmod(n_space - d, CORES)
        return lax.rem(xi + over, nx) * CORES + lax.rem(core + flip, CORES)

    def x_at(d):
        return lax.rem(xi + d + nx, nx) * CORES + core

    def pair(d):
        p = me
        bit = 1
        while bit < n_mem:
            if d & bit:
                p = p + bit - 2 * bit * lax.rem(lax.div(me, bit), 2)
            bit *= 2
        return p

    def cols(p):
        return pl.ds(pl.multiple_of(p * variables, variables), variables)

    def block_rows(p):
        return rows_at(p * block, block)

    def chunk_rows(c):
        return pl.ds(c * rows, rows)

    def sample_rows(p):
        return rows_at(p * samples, samples)

    loads = [
        pltpu.make_async_copy(prior.at[:, cols(me)], x.at[sp, block_rows(me), :], local.at[0]),
        pltpu.make_async_copy(terminal.at[sample_rows(sp), :], z.at[:, cols(sp)], local.at[1]),
        pltpu.make_async_copy(angles, seen.at[:, cols(sp)], local.at[2]),
        pltpu.make_async_copy(
            perturbation.at[:, sample_rows(sp), :], noise.at[:, :, cols(sp)], local.at[3]
        ),
    ]
    for copy in loads:
        copy.start()

    barrier = pltpu.get_barrier_semaphore()
    greet = [(space_at(d), me) for d in range(1, n_space)]
    greet += [(sp, pair(d)) for d in range(1, n_mem)]
    for dev in greet:
        pl.semaphore_signal(barrier, inc=1, device_id=dev, device_id_type=MESH)
    pl.semaphore_wait(barrier, len(greet))

    together = max(1, LANES // block)
    groups = range(n_mem // together)
    slots = {}
    pending = {}

    def copy_at(key, src, dst, dev):
        i = slots.setdefault(key, len(slots))
        return pltpu.make_async_remote_copy(
            src_ref=src,
            dst_ref=dst,
            send_sem=send.at[i],
            recv_sem=recv.at[i],
            device_id=dev,
            device_id_type=MESH,
        )

    def put(key, src, dst, dev):
        return put_all(key, [(src, dst, dev)], dst)

    def put_all(key, copies, landing):
        if key in pending:
            pending[key].wait_send()
        for src, dst, dev in copies:
            copy_at(key, src, dst, dev).start()
        pending[key] = copy_at(key, landing, landing, copies[0][2])
        return pending[key]

    here = x.at[sp, block_rows(me), :]
    others = pl.ds(0, (n_space - 1) * variables)
    exchange = {
        d: put(("mem", d), prior.at[:, cols(pair(d))], here, (sp, pair(d)))
        for d in range(1, n_mem)
    }

    def send_start(c):
        copies = []
        for d in range(1, n_space):
            q = space_at(d)
            src = terminal.at[rows_at(q * samples + c * rows, rows), :]
            copies.append((src, z.at[chunk_rows(c), cols(sp)], (q, me)))
        return put_all(("space", c), copies, z.at[chunk_rows(c), others])

    starts = [send_start(0)]

    over_x, to_core, onward = [], [], []

    def group_at(i):
        return rows_at(lax.div(pair(i * together), together) * together * block, together * block)

    def group_blocks(i):
        return range(i * together, (i + 1) * together)

    def pass_on(b, src, at):
        over_x.append(
            [put(("x", b, d), src, at, (x_at(d), me)) for d in range(1, nx)]
        )

    def pass_core(i):
        for b in group_blocks(i):
            for copy in over_x[b]:
                copy.wait_recv()
        onward.append([])
        for d in range(1, nx):
            at = x.at[x_at(-d), group_at(i), :]
            onward[i].append(put(("onward", i, d), at, at, partner))

    def take(q, i):
        some = group_at(i)
        xs = x[q, some, :]
        for j, piece in enumerate(split(xs, PARTS)):
            xb[j, some, cols(q)] = piece
        turned = xs.T
        for j, piece in enumerate(split(turned, PARTS)):
            xt[j, cols(q), some] = piece
        norms[:, some] = norms[:, some] + jnp.sum(turned * turned, axis=0, keepdims=True)

    norms[...] = jnp.zeros_like(norms)
    pass_on(0, prior.at[:, cols(me)], here)
    loads[0].wait()
    for i in groups:
        for d in group_blocks(i):
            if d:
                exchange[d].wait_recv()
                at = x.at[sp, block_rows(pair(d)), :]
                pass_on(d, at, at)
        at = x.at[sp, group_at(i), :]
        to_core.append(put(("core", i), at, at, partner))
        take(sp, i)
    starts += [send_start(c) for c in range(1, chunks)]
    firsts = put_all(
        "angles",
        [(angles, seen.at[:, cols(sp)], (space_at(d), me)) for d in range(1, n_space)],
        seen.at[:, others],
    )
    for copy in loads[1:3]:
        copy.wait()

    inbound = {}

    owned = me if scatter else 0

    def send_noise(k):
        copies = []
        for d in range(1, n_space):
            q = space_at(d)
            src = perturbation.at[k, sample_rows(q), :]
            copies.append((src, noise.at[k, :, cols(sp)], (q, me)))
        return put_all(("noise", k), copies, noise.at[k, :, others])

    def send_sums(k, c, i=None):
        alpha = constants(k)[1]
        some = pl.ds(0, members) if i is None else group_at(i)
        parts = [xt[j, :, some] for j in range(PARTS)]
        inner = product(z[chunk_rows(c), :], parts, 0)
        value = 2.0 * alpha * inner - alpha * alpha * norms[:, some]
        gram[k, c, :, :, some] = value.reshape(pieces, own_rows, value.shape[1])
        copies = []
        for d in reversed(range(1, n_mem)):
            src = gram.at[k, c, pair(d) if scatter else 0, :, some]
            copies.append((src, sums.at[k, c, d - 1, :, some], (sp, pair(d))))
        landing = sums.at[k, c, :, :, some]
        inbound["sums", k, c].append(put_all(("sums", c, i or 0), copies, landing))

    def send_weights(k, c):
        total = gram[k, c, owned]
        for copy in inbound["sums", k, c]:
            copy.wait_recv()
        for d in range(n_mem - 1):
            total = total + sums[k, c, d]
        logits = total / (2.0 * constants(k)[0] * temper)
        e = jnp.exp(logits - jnp.max(logits, axis=1, keepdims=True))
        w[k, c, owned] = e / jnp.sum(e, axis=1, keepdims=True)
        if scatter:
            at = w.at[k, c, owned]
            copies = [(at, at, (sp, pair(d))) for d in reversed(range(1, n_mem))]
            landing = w.at[k, c, pl.ds(0, n_mem - 1)]
            inbound["give", k, c] = put_all(("give", c), copies, landing)

    def advance(k, c):
        t, alpha, drift, g2, damp = constants(k)
        zs = z[chunk_rows(c), :]
        seen_term = damp * 4.0 * (seen[...] - arctan(zs)) / (1.0 + zs * zs)
        z[chunk_rows(c), :] = (
            zs
            + dt * (-drift * zs + g2 * (seen_term - zs / t))
            + math.sqrt(dt * g2) * noise[k, chunk_rows(c), :]
        )

    def add_blend(k, c):
        t, alpha, _, g2, _ = constants(k)
        if scatter:
            inbound["give", k, c].wait_recv()
        blend = product(w[k, c].reshape(rows, members), [xb[j] for j in range(PARTS)], 0)
        z[chunk_rows(c), :] = z[chunk_rows(c), :] + (dt * g2 * alpha / t) * blend

    each = list(range(chunks))
    results = []
    arriving = {}
    for k in range(ITERS):
        for c in each:
            inbound["sums", k, c] = []
    starts[0].wait_recv()

    def finish_group(i):
        for copy in onward[i]:
            copy.wait_recv()
        for d in range(1, nx):
            take(lax.rem(xi + d, nx) * CORES + 1 - core, i)
        send_sums(0, 0, i)

    for i in groups:
        pass_core(i)
        for d in range(1, nx):
            take(x_at(d), i)
        to_core[i].wait_recv()
        take(xi * CORES + 1 - core, i)
        if i:
            finish_group(i - 1)
    finish_group(len(groups) - 1)
    for k in range(ITERS):
        for c in each:
            if k > 0:
                add_blend(k - 1, c)
            elif c > 0:
                starts[c].wait_recv()
            if k + c > 0:
                send_sums(k, c)
        if k == 0:
            arriving[0] = send_noise(0)
        for c in each:
            send_weights(k, c)
        if k + 1 < ITERS:
            arriving[k + 1] = send_noise(k + 1)
        if k == 0:
            loads[3].wait()
            firsts.wait_recv()
        arriving[k].wait_recv()
        for c in each:
            advance(k, c)
    for c in each:
        add_blend(ITERS - 1, c)
        target = out.at[rows_at(sp * samples + c * rows, rows), :]
        copies = []
        for d in range(1, n_space):
            q = space_at(d)
            copies.append((z.at[chunk_rows(c), cols(q)], target, (q, me)))
        results.append(put_all(("space", c), copies, z.at[chunk_rows(c), others]))
        own = pltpu.make_async_copy(z.at[chunk_rows(c), cols(sp)], target, local.at[4 + c])
        own.start()
        loads.append(own)
    for copy in loads[4:]:
        copy.wait()
    for copy in results:
        copy.wait_recv()
    for copy in pending.values():
        copy.wait_send()


def per_device(prior, terminal, perturbation, angles):
    n_space, n_mem = lax.axis_size("space"), lax.axis_size("mem")
    all_samples, variables = terminal.shape
    members = prior.shape[0] * n_mem
    samples = all_samples // n_space
    chunks = CHUNKS
    while chunks > 1 and samples % (chunks * n_mem * PIECE):
        chunks //= 2
    rows = samples // chunks
    scatter = rows % (n_mem * PIECE) == 0
    pieces = n_mem if scatter else 1
    own_rows = rows // pieces
    block = prior.shape[0]
    groups = n_mem // max(1, LANES // block)
    wide = n_space * variables
    assert n_mem & (n_mem - 1) == 0
    temper = math.sqrt(wide * n_mem)
    f32 = jnp.float32
    nx = n_space // CORES
    iters = perturbation.shape[0]
    slots = n_mem - 1 + n_mem * (nx - 1) + groups * (nx + 1) + 3 * chunks + iters
    operands = prior, terminal, perturbation, angles.reshape(1, variables)
    anywhere = pl.BlockSpec(memory_space=pl.ANY)
    return pl.pallas_call(
        functools.partial(kernel, (n_space, n_mem, scatter, temper)),
        out_shape=jax.ShapeDtypeStruct((all_samples, variables), f32),
        in_specs=[anywhere] * 4,
        out_specs=anywhere,
        scratch_shapes=[
            pltpu.VMEM((n_space, members, variables), f32),
            pltpu.VMEM((samples, wide), f32),
            pltpu.VMEM((iters, samples, wide), f32),
            pltpu.VMEM((1, wide), f32),
            pltpu.VMEM((iters, chunks, pieces, own_rows, members), f32),
            pltpu.VMEM((iters, chunks, n_mem - 1, own_rows, members), f32),
            pltpu.VMEM((iters, chunks, pieces, own_rows, members), f32),
            pltpu.VMEM((PARTS, members, wide), jnp.bfloat16),
            pltpu.VMEM((PARTS, wide, members), jnp.bfloat16),
            pltpu.VMEM((1, members), f32),
            pltpu.SemaphoreType.DMA((slots,)),
            pltpu.SemaphoreType.DMA((slots,)),
            pltpu.SemaphoreType.DMA((4 + chunks,)),
        ],
        compiler_params=pltpu.CompilerParams(
            collective_id=0, has_side_effects=True, vmem_limit_bytes=VMEM_LIMIT
        ),
    )(*[pltpu.with_memory_space_constraint(a, pltpu.HBM) for a in operands])


def solution(mesh):
    in_specs = (
        P("mem", "space"),
        P(None, ("space", "mem")),
        P(None, None, ("space", "mem")),
        P(("space", "mem")),
    )
    out_specs = P(None, ("space", "mem"))
    return jax.shard_map(
        per_device, mesh=mesh, in_specs=in_specs, out_specs=out_specs, check_vma=False
    )
```
